32 devices in a mesh: row: 4 (over y, core), col: 8 (over z, x).
Axes of the slice: x: 2, y: 2, z: 4, core: 2. Of those that a mesh axis runs over, the one named last changes fastest.
Arguments:
- cov: float32 [16384, 16384], P('row', 'col'), may hold values from -40 to 40, as said below
- noise: float32 [16384, 16384], P('row', 'col'), may hold values from -12 to 12, as said below
- velocity_x: float32 [128, 128], replicated, may hold values from -0.8 to 0.8
- velocity_y: float32 [128, 128], replicated, may hold values from -0.8 to 0.8
- diffusion: float32 [128, 128], replicated, may hold values from 0.05 to 0.25
Outputs:
- forecast: float32 [16384, 16384], P('row', 'col')
The draws below stay inside these ranges and needn't reach their ends.
Inputs may be any that keep to these rules, and one draw needn't show every extreme that they name: `cov`: symmetric, its diagonal lifted by 2. `noise`: symmetric, its diagonal lifted by 0.5.
All inputs are finite; a program needn't handle non-finite values.
Results may differ from the reference program's by a relative error of at most 0.000061.
Values sent between devices are 32-bit elements; how exact they have to be, the bound alone decides.
No kernel may reach another device: no remote copies, remote signals or barrier semaphores. Data moves between devices by JAX's collectives and lax.ppermute only.
A program may use at most 384 MiB of HBM per device.

```python
import math
import jax
import jax.numpy as jnp
from jax import lax

NLAT = 128
NLON = 128
N = 16384


def symmetric_draw(key, scale, lift):
    base = jax.random.truncated_normal(key, -4.0, 4.0, (N, N), jnp.float32)
    sym = (base + base.T) * (0.5 * scale)
    return sym + lift * jnp.eye(N, dtype=jnp.float32)


def draw_cov(key, part):
    return symmetric_draw(jax.random.fold_in(key, 11), 1.0, 2.0)


def draw_noise(key, part):
    return symmetric_draw(jax.random.fold_in(key, 23), 0.3, 0.5)


def setup_inputs(seed: int = 0) -> dict:
    arg_keys = jax.random.split(jax.random.key(seed), 6)
    return {
        "cov": draw_cov(jax.random.fold_in(arg_keys[5], 71), 0),
        "noise": draw_noise(jax.random.fold_in(arg_keys[5], 71), 0),
        "velocity_x": jnp.clip(jax.random.uniform(arg_keys[2], (NLAT, NLON), jnp.float32, -0.8, 0.8), -0.8, 0.8),
        "velocity_y": jnp.clip(jax.random.uniform(arg_keys[3], (NLAT, NLON), jnp.float32, -0.8, 0.8), -0.8, 0.8),
        "diffusion": jnp.clip(jnp.exp(jax.random.uniform(arg_keys[4], (NLAT, NLON), jnp.float32, math.log(0.05), math.log(0.25))), 0.05, 0.25),
    }


third = 1.0 / 3.0
two_thirds = 2.0 / 3.0


def tendency(extended, kappa, vel_x, vel_y, axis):
    rows = extended.shape[axis] - 2
    centre = lax.slice_in_dim(extended, 1, rows + 1, axis=axis)
    north = lax.slice_in_dim(extended, 2, rows + 2, axis=axis)
    south = lax.slice_in_dim(extended, 0, rows, axis=axis)
    east = jnp.roll(centre, -1, axis + 1)
    west = jnp.roll(centre, 1, axis + 1)
    return kappa * (east + west + north + south - 4.0 * centre) - 0.5 * vel_x * (east - west) - 0.5 * vel_y * (north - south)


def apply_step(field, kappa, vel_x, vel_y, axis):
    def padded(value):
        widths = [(0, 0)] * value.ndim
        widths[axis] = (1, 1)
        return jnp.pad(value, widths)

    first = field + tendency(padded(field), kappa, vel_x, vel_y, axis)
    second = 0.75 * field + 0.25 * (first + tendency(padded(first), kappa, vel_x, vel_y, axis))
    return third * field + two_thirds * (second + tendency(padded(second), kappa, vel_x, vel_y, axis))


def reference(cov, noise, velocity_x, velocity_y, diffusion):
    size = NLAT * NLON
    count = 16
    rows = size // count

    def along_last(block):
        shaped = block.reshape(rows, NLAT, NLON)
        return apply_step(shaped, diffusion, velocity_x, velocity_y, 1).reshape(rows, size)

    half = lax.map(along_last, cov.reshape(count, rows, size)).reshape(size, size)
    state = half.reshape(NLAT, NLON, size)

    def along_first(index):
        piece = lax.dynamic_slice_in_dim(state, index * rows, rows, 2)
        return apply_step(piece, diffusion[:, :, None], velocity_x[:, :, None], velocity_y[:, :, None], 0)

    blocks = lax.map(along_first, jnp.arange(count, dtype=jnp.int32))
    full = jnp.moveaxis(blocks, 0, 2).reshape(size, size)
    return full + noise
```

```python
import functools
import random

import jax
import jax.numpy as jnp
from jax import lax
from jax.experimental import pallas as pl
from jax.experimental.pallas import tpu as pltpu
from jax.sharding import PartitionSpec as P

VMEM_LIMIT = 62 * 1024 * 1024
SUBLANES = 8
COL_ROWS = 128
third = 1.0 / 3.0


WIDTH = 3
SWEEPS = 400


def route(source, target):
    (sr, sc, xs), (tr, tc, _) = source, target
    steps = []
    here = [sc // xs, sc % xs, sr // 2]
    goal = [tc // xs, tc % xs, tr // 2]
    for axis in range(3):
        while here[axis] != goal[axis]:
            step = 1 if goal[axis] > here[axis] else -1
            steps.append((tuple(here), axis, step))
            here[axis] += step
    return steps


def halo_plan(rows, cols, lat_row, lat_col):
    xs = max(cols // 4, 1)
    piece = min(lat_row, lat_col)
    parts = lat_row // piece
    wants = []
    for r in range(rows):
        for c in range(cols):
            for side in range(2):
                near = c - 1 + 2 * side
                if not 0 <= near < cols:
                    continue
                lat_j = c * lat_col - WIDTH if side == 0 else (c + 1) * lat_col
                for part in range(parts):
                    lat_i = r * lat_row + part * piece
                    direct = ((r, near), (0, part * piece, lat_j % lat_col))
                    mirror = (
                        (lat_j // lat_row, lat_i // lat_col),
                        (1, lat_j % lat_row, lat_i % lat_col),
                    )
                    options = []
                    for (sr, sc), where in (direct, mirror):
                        options.append(((sr, sc), where, route((sr, sc, xs), (r, c, xs))))
                    wants.append(((r, c), (side, part), options))
    load = {}
    for r in range(rows - 1):
        for c in range(cols):
            for a, b in (((r, c, xs), (r + 1, c, xs)), ((r + 1, c, xs), (r, c, xs))):
                for link in route(a, b):
                    load[link] = load.get(link, 0) + 1
    degree = {}
    limit = 2 * parts

    rng = random.Random(0)
    pick = [0] * len(wants)

    def put(option, sign):
        source, _, links = option
        for link in links:
            load[link] = load.get(link, 0) + sign
        degree[source] = degree.get(source, 0) + sign

    def price(option, weight):
        source, _, links = option
        cost = sum((load.get(k, 0) + 1) ** 6 - load.get(k, 0) ** 6 for k in links)
        return cost + weight * max(degree.get(source, 0) + 1 - limit, 0)

    def score():
        over = sum(max(n - limit, 0) for n in degree.values())
        return over, sum(n**6 for n in load.values())

    for _, _, options in wants:
        put(options[0], 1)
    best, kept = score(), list(pick)
    for sweep in range(SWEEPS):
        heat = 1.0 - (sweep % 100) / 100
        order = list(range(len(wants)))
        rng.shuffle(order)
        for n in order:
            options = wants[n][2]
            put(options[pick[n]], -1)
            costs = [price(o, 8000.0) + 6000.0 * heat * rng.random() for o in options]
            pick[n] = costs.index(min(costs))
            put(options[pick[n]], 1)
        now = score()
        if now < best:
            best, kept = now, list(pick)
    chosen = []
    for n, (target, slot, options) in enumerate(wants):
        source, where, links = options[kept[n]]
        chosen.append((source, target, slot, where, links))
    return chosen, piece, parts


def colour(edges):
    at_source, at_target, result = {}, {}, {}
    degree = {}
    for source, target in edges:
        degree[("s", source)] = degree.get(("s", source), 0) + 1
        degree[("t", target)] = degree.get(("t", target), 0) + 1
    rounds = max(degree.values())
    for n, (source, target) in enumerate(edges):
        used_s = at_source.setdefault(source, {})
        used_t = at_target.setdefault(target, {})
        a = next(k for k in range(rounds) if k not in used_s)
        b = next(k for k in range(rounds) if k not in used_t)
        if a != b:
            chain, side, node, want = [], "t", target, a
            while True:
                table = at_target[node] if side == "t" else at_source[node]
                if want not in table:
                    break
                edge = table[want]
                chain.append(edge)
                node = edges[edge][0] if side == "t" else edges[edge][1]
                side = "s" if side == "t" else "t"
                want = b if want == a else a
            for edge in chain:
                s, t = edges[edge]
                del at_source[s][result[edge]], at_target[t][result[edge]]
            for edge in chain:
                s, t = edges[edge]
                result[edge] = b if result[edge] == a else a
                at_source[s][result[edge]] = edge
                at_target[t][result[edge]] = edge
        result[n] = a
        used_s[a] = n
        used_t[a] = n
    return rounds, [result[n] for n in range(len(edges))]


def pack_kernel(parts, lanes, step_lats, where, cov, out, straight, turned, sems):
    flip, row, col = where[0], where[1], where[2]
    width = WIDTH * lanes
    span = step_lats * lanes
    row = pl.multiple_of(row * lanes, lanes)
    col = pl.multiple_of(col * lanes, lanes)

    def copies(n):
        return (
            pltpu.make_async_copy(
                cov.at[pl.ds(row + n * span, span), pl.ds(col, width)],
                straight.at[pl.ds(n * span, span), :],
                sems.at[n],
            ),
            pltpu.make_async_copy(
                cov.at[pl.ds(row, width), pl.ds(col + n * span, span)],
                turned.at[:, pl.ds(n * span, span)],
                sems.at[n],
            ),
        )

    for n in range(parts):
        plain, flipped = copies(n)
        pl.when(flip == 0)(plain.start)
        pl.when(flip == 1)(flipped.start)
    for n in range(parts):
        plain, flipped = copies(n)

        @pl.when(flip == 0)
        def _():
            plain.wait()
            for a in range(step_lats):
                lat = n * step_lats + a
                out[lat] = straight[lat * lanes : (lat + 1) * lanes, :]

        @pl.when(flip == 1)
        def _():
            flipped.wait()
            for a in range(step_lats):
                lat = n * step_lats + a
                for b in range(WIDTH):
                    tile = turned[b * lanes : (b + 1) * lanes, lat * lanes : (lat + 1) * lanes]
                    out[lat, :, b * lanes : (b + 1) * lanes] = tile.T


def pack(where, cov, piece, lanes):
    parts = max(piece // 4, 1)
    step = piece // parts
    return pl.pallas_call(
        functools.partial(pack_kernel, parts, lanes, step),
        out_shape=jax.ShapeDtypeStruct((piece, lanes, WIDTH * lanes), cov.dtype),
        in_specs=[
            pl.BlockSpec(memory_space=pltpu.SMEM),
            pl.BlockSpec(memory_space=pl.ANY),
        ],
        out_specs=pl.BlockSpec(memory_space=pltpu.VMEM),
        scratch_shapes=[
            pltpu.VMEM((piece * lanes, WIDTH * lanes), cov.dtype),
            pltpu.VMEM((WIDTH * lanes, piece * lanes), cov.dtype),
            pltpu.SemaphoreType.DMA((parts,)),
        ],
        compiler_params=pltpu.CompilerParams(vmem_limit_bytes=VMEM_LIMIT),
        cost_estimate=pl.CostEstimate(
            flops=0, bytes_accessed=8 * piece * lanes * WIDTH * lanes, transcendentals=0
        ),
        name="pack",
    )(where, cov)


def row_step(strips, fields, slots, lats, row_coefs, half):
    source, one, two = fields
    (c0, c1, c2, c3), (f1, f2, f3), (g1, g2, g3) = slots
    lanes = half.shape[1]
    tiles = lanes // SUBLANES
    place = lax.broadcasted_iota(jnp.int32, (SUBLANES, half.shape[2]), 0)
    top, bottom = place == SUBLANES - 1, place == 0

    @pl.loop(0, strips)
    def _(s):
        def tile(field, slot, r):
            return field[slot, s, r * SUBLANES : (r + 1) * SUBLANES, :]

        def turns(field, slot, r):
            here = tile(field, slot, r)
            return here, pltpu.roll(here, SUBLANES - 1, 0), pltpu.roll(here, 1, 0)

        def weigh(stage, r, around, north, south):
            last, (here, up, down), following = around
            coefs = [
                row_coefs[lats[stage], k, r * SUBLANES : (r + 1) * SUBLANES, :] for k in range(5)
            ]
            east = jnp.where(top, following[1], up)
            west = jnp.where(bottom, last[2], down)
            return (
                coefs[0] * east
                + coefs[1] * west
                + coefs[2] * north
                + coefs[3] * south
                + coefs[4] * here
            )

        rolled = [(source, c1), (one, f2), (two, g2)]
        start = [[turns(*f, tiles - 1), turns(*f, 0)] for f in rolled]
        around = [list(w) for w in start]
        for r in range(tiles):
            span = slice(r * SUBLANES, (r + 1) * SUBLANES)
            for n, f in enumerate(rolled):
                around[n].append(start[n][1] if r + 1 == tiles else turns(*f, r + 1))
            mid = tile(source, c2, r)
            v1 = around[0][1][0] + third * weigh(0, r, around[0], tile(source, c0, r), mid)
            v2 = mid + 0.5 * weigh(1, r, around[1], v1, tile(one, f3, r))
            half[s, span, :] = tile(source, c3, r) + weigh(
                2, r, around[2], v2, tile(two, g3, r)
            )
            one[f1, s, span, :] = v1
            two[g1, s, span, :] = v2
            for w in around:
                del w[0]


def ring_slots(step):
    field = [lax.rem(step + 4 - back, 4) for back in range(4)]
    one = [lax.rem(step + 6 - back, 3) for back in range(3)]
    return field, one, one


def col_stage(fields, lat, weights, mixers):
    total = None
    if lat in fields:
        here = fields[lat]
        lanes = here.shape[1]
        coarse = here.astype(jnp.bfloat16)
        fine = (here - coarse.astype(jnp.float32)).astype(jnp.bfloat16)
        both = jnp.dot(
            jnp.concatenate([coarse, fine], axis=1),
            mixers[lat + 2],
            preferred_element_type=jnp.float32,
        )
        total = both[:, :lanes] + both[:, lanes:]
    for step, k in ((1, 2), (-1, 3)):
        if lat + step in fields:
            value = weights[lat + 2, k : k + 1, :] * fields[lat + step]
            total = value if total is None else total + value
    return total


def plus(fields, lat, value):
    return fields[lat] + value if lat in fields else value


def stream_kernel(plan, lat_col, lanes, *refs):
    sources = refs[: plan.sources]
    noise, row_coefs, col_coefs, mixers = refs[plan.sources : plan.sources + 4]
    out, ring, one, two, half, first, second = refs[-7:]
    step = pl.program_id(0)
    local = plan.local(step)
    slots = ring_slots(step)

    for source, when in zip(sources, plan.which(step)):

        @pl.when(when)
        def _():
            slot = slots[0][0]
            for s in range(lat_col):
                ring[slot, s] = source[:, s * lanes : (s + 1) * lanes]

    @pl.when(local >= 2)
    def _():
        lats = [jnp.maximum(plan.lat(step) + WIDTH - back, 0) for back in (1, 2, 3)]
        row_step(lat_col, (ring, one, two), slots, lats, row_coefs, half)

    @pl.when(local >= 2 * WIDTH)
    def _():
        @pl.loop(0, lanes // COL_ROWS)
        def _(n):
            rows = pl.ds(pl.multiple_of(n * COL_ROWS, COL_ROWS), COL_ROWS)
            u = Stored(half, rows, 0, range(lat_col))
            v = Stored(first, rows, 1, [])
            w = Stored(second, rows, 1, [])
            for lat in range(-1, lat_col + 3):
                if lat <= lat_col:
                    v[lat] = plus(u, lat, third * col_stage(u, lat, col_coefs, mixers))
                at = lat - 1
                if -1 <= at <= lat_col:
                    w[at] = plus(u, at, 0.5 * col_stage(v, at, col_coefs, mixers))
                at = lat - 2
                if 0 <= at < lat_col:
                    span = slice(at * lanes, (at + 1) * lanes)
                    value = u[at] + col_stage(w, at, col_coefs, mixers)
                    out[rows, span] = value + noise[rows, span]


class Stored:
    def __init__(self, ref, rows, shift, lats):
        self.ref, self.rows, self.shift, self.lats = ref, rows, shift, set(lats)

    def __contains__(self, lat):
        return lat in self.lats

    def __getitem__(self, lat):
        return self.ref[lat + self.shift, self.rows, :]

    def __setitem__(self, lat, value):
        self.lats.add(lat)
        self.ref[lat + self.shift, self.rows, :] = value


class Inner:
    sources = 1

    def __init__(self, lats):
        self.lats = lats
        self.steps = lats

    def local(self, step):
        return step

    def lat(self, step):
        return step

    def which(self, step):
        return (step >= 0,)

    def inputs(self):
        return (lambda n: (n, 0),)

    def output(self, step):
        return (jnp.clip(step - WIDTH, WIDTH, self.lats - WIDTH - 1), 0)


class Ends:
    sources = 3

    def __init__(self, lats):
        self.lats = lats
        self.steps = 6 * WIDTH

    def local(self, step):
        return lax.rem(step, 3 * WIDTH)

    def lat(self, step):
        upper = step >= 3 * WIDTH
        return jnp.where(upper, self.lats - 5 * WIDTH + step, step - WIDTH)

    def which(self, step):
        lat = self.lat(step)
        return lat < 0, (lat >= 0) & (lat < self.lats), lat >= self.lats

    def inputs(self):
        def low(n):
            return (jnp.minimum(n, WIDTH - 1), 0)

        def own(n):
            return (jnp.clip(self.lat(n), 0, self.lats - 1), 0)

        def high(n):
            return (jnp.clip(self.lat(n) - self.lats, 0, WIDTH - 1), 0)

        return low, own, high

    def output(self, step):
        upper = step >= 3 * WIDTH
        back = jnp.maximum(self.local(step) - 2 * WIDTH, 0)
        return (jnp.where(upper, self.lats - WIDTH, 0) + back, 0)


def stream(plan, sources, noise, row_coefs, col_coefs, mixers, lanes, kept=None):
    rows, cols = noise.shape
    lat_col = cols // lanes
    band = (lanes, cols)
    tall = (lat_col, lanes, lanes)
    extra, aliases = (), {}
    extra_specs = []
    if kept is not None:
        extra = (kept,)
        extra_specs = [pl.BlockSpec(memory_space=pl.ANY)]
        aliases = {plan.sources + 4: 0}
    work = rows * cols * plan.steps // (rows // lanes)
    return pl.pallas_call(
        functools.partial(stream_kernel, plan, lat_col, lanes),
        grid=(plan.steps,),
        out_shape=jax.ShapeDtypeStruct(noise.shape, noise.dtype),
        in_specs=[pl.BlockSpec(band, index) for index in plan.inputs()]
        + [
            pl.BlockSpec(band, plan.output),
            pl.BlockSpec(memory_space=pltpu.VMEM),
            pl.BlockSpec(memory_space=pltpu.VMEM),
            pl.BlockSpec(memory_space=pltpu.VMEM),
        ]
        + extra_specs,
        out_specs=pl.BlockSpec(band, plan.output),
        scratch_shapes=[
            pltpu.VMEM((4,) + tall, noise.dtype),
            pltpu.VMEM((3,) + tall, noise.dtype),
            pltpu.VMEM((3,) + tall, noise.dtype),
            pltpu.VMEM((lat_col, lanes, lanes), noise.dtype),
            pltpu.VMEM((lat_col + 2, lanes, lanes), noise.dtype),
            pltpu.VMEM((lat_col + 2, lanes, lanes), noise.dtype),
        ],
        input_output_aliases=aliases,
        compiler_params=pltpu.CompilerParams(
            vmem_limit_bytes=VMEM_LIMIT, dimension_semantics=("arbitrary",)
        ),
        cost_estimate=pl.CostEstimate(
            flops=70 * work, bytes_accessed=12 * work, transcendentals=0
        ),
        name=type(plan).__name__.lower(),
    )(*sources, noise, row_coefs, col_coefs, mixers, *extra)


def corner_kernel(count, parts, width, slots, *refs):
    got, (first, last, sem) = refs[:count], refs[count:]
    piece = got[0].shape[0]
    for go in (0, 1):
        for side in range(2):
            for end, ref, lat in ((0, first, 0), (parts - 1, last, piece - WIDTH)):
                slot = slots[side * parts + end]
                target = ref.at[:, :, pl.ds(side * width, width)]
                for n in range(count):

                    @pl.when(slot == n)
                    def _():
                        copy = pltpu.make_async_copy(
                            got[n].at[pl.ds(lat, WIDTH)], target, sem.at[2 * side + (ref is last)]
                        )
                        copy.wait() if go else copy.start()

                if not go:

                    @pl.when(slot < 0)
                    def _():
                        target[...] = jnp.zeros(target.shape, target.dtype)


def corners(slots, got, parts):
    piece, lanes, width = got[0].shape
    shape = jax.ShapeDtypeStruct((WIDTH, lanes, 2 * width), got[0].dtype)
    return pl.pallas_call(
        functools.partial(corner_kernel, len(got), parts, width),
        out_shape=(shape, shape),
        in_specs=[pl.BlockSpec(memory_space=pltpu.SMEM)]
        + [pl.BlockSpec(memory_space=pl.ANY)] * len(got),
        out_specs=(pl.BlockSpec(memory_space=pltpu.VMEM),) * 2,
        scratch_shapes=[pltpu.SemaphoreType.DMA((4,))],
        compiler_params=pltpu.CompilerParams(vmem_limit_bytes=VMEM_LIMIT),
        name="corners",
    )(slots, *got)


def rim_kernel(count, parts, lats, lat_col, lanes, slots, *refs):
    got = refs[:count]
    low, high, row_coefs_hbm, col_coefs, mixers, _, out = refs[count : count + 7]
    halo, edge, row_coefs, one, two, half, got_sem, end_sem, in_sem, out_sem, coef_sem = refs[
        count + 7 :
    ]
    piece = lats // parts
    width = WIDTH * lanes
    tall = lats + 2 * WIDTH

    coef_copy = pltpu.make_async_copy(row_coefs_hbm, row_coefs, coef_sem)

    def strip_of(field, strip):
        return field.at[:, :, pl.ds(strip * lanes, lanes)]

    def place(first, depth, strip):
        return halo.at[pl.ds(first, depth), strip]

    def end_copies():
        for n in range(2 * WIDTH):
            yield pltpu.make_async_copy(strip_of(low, n), place(0, WIDTH, n), end_sem)
            yield pltpu.make_async_copy(strip_of(high, n), place(WIDTH + lats, WIDTH, n), end_sem)

    def each_piece(part, go):
        for side in range(2):
            slot = slots[side * parts + part]
            first = WIDTH + part * piece
            for n in range(count):

                @pl.when(slot == n)
                def _():
                    for k in range(WIDTH):
                        copy = pltpu.make_async_copy(
                            strip_of(got[n], k),
                            place(first, piece, side * WIDTH + k),
                            got_sem.at[side, part],
                        )
                        copy.wait() if go else copy.start()

            if not go:

                @pl.when(slot < 0)
                def _():
                    for k in range(WIDTH):
                        target = place(first, piece, side * WIDTH + k)
                        target[...] = jnp.zeros(target.shape, target.dtype)

    def edge_copy(side, part, inward):
        outside = out.at[
            pl.ds(part * piece, piece), :, pl.ds(side * (lat_col - WIDTH) * lanes, width)
        ]
        inside = edge.at[pl.ds(part * piece, piece), :, pl.ds(side * width, width)]
        if inward:
            return pltpu.make_async_copy(outside, inside, in_sem.at[side, part])
        return pltpu.make_async_copy(inside, outside, out_sem.at[side, part])

    for copy in end_copies():
        copy.start()
    for part in range(parts):
        each_piece(part, False)
        if part == 0:
            coef_copy.start()
        for side in range(2):
            edge_copy(side, part, True).start()
    for copy in end_copies():
        copy.wait()
    coef_copy.wait()

    def one_lat(step):
        _, early, later = ring_slots(step)

        @pl.when(step >= 2)
        def _():
            back = [jnp.maximum(step - n, 0) for n in range(4)]
            row_step(
                2 * WIDTH, (halo, one, two), (back, early, later), back[1:], row_coefs, half
            )

        @pl.when(step >= 2 * WIDTH)
        def _():
            @pl.loop(0, lanes // COL_ROWS)
            def _(n):
                rows = pl.ds(pl.multiple_of(n * COL_ROWS, COL_ROWS), COL_ROWS)

                for side in range(2):
                    def at(d):
                        return d if side == 0 else lat_col - 1 - d

                    u = {}
                    for d in range(-WIDTH, 0):
                        strip = d + WIDTH if side == 0 else WIDTH - d - 1
                        u[at(d)] = half[strip, rows, :]
                    v = {
                        at(d): plus(u, at(d), third * col_stage(u, at(d), col_coefs, mixers))
                        for d in (-2, -1, 0)
                    }
                    w = {
                        at(d): plus(u, at(d), 0.5 * col_stage(v, at(d), col_coefs, mixers))
                        for d in (-1, 0, 1)
                    }
                    for d in range(WIDTH):
                        start = side * width + (d if side == 0 else WIDTH - 1 - d) * lanes
                        span = slice(start, start + lanes)
                        lat = step - 2 * WIDTH
                        value = col_stage(w, at(d), col_coefs, mixers)
                        edge[lat, rows, span] = edge[lat, rows, span] + value

    bounds = [0] + [WIDTH + (p + 1) * piece for p in range(parts - 1)] + [tall]
    for part in range(parts):
        each_piece(part, True)
        for side in range(2):
            edge_copy(side, part, True).wait()

        @pl.loop(bounds[part], bounds[part + 1])
        def _(step):
            one_lat(step)

        if part > 0:
            for side in range(2):
                edge_copy(side, part - 1, False).start()
    for side in range(2):
        edge_copy(side, parts - 1, False).start()
    for part in range(parts):
        for side in range(2):
            edge_copy(side, part, False).wait()


def rim(slots, got, low, high, row_coefs, col_coefs, mixers, forecast, parts, lanes):
    rows, cols = forecast.shape
    lats, lat_col = rows // lanes, cols // lanes
    count = len(got)
    width = WIDTH * lanes
    kept = forecast.reshape(lats, lanes, cols)
    tall = (2 * WIDTH, lanes, lanes)
    result = pl.pallas_call(
        functools.partial(rim_kernel, count, parts, lats, lat_col, lanes),
        out_shape=jax.ShapeDtypeStruct(kept.shape, kept.dtype),
        in_specs=[pl.BlockSpec(memory_space=pltpu.SMEM)]
        + [pl.BlockSpec(memory_space=pl.ANY)] * count
        + [
            pl.BlockSpec(memory_space=pl.ANY),
            pl.BlockSpec(memory_space=pl.ANY),
            pl.BlockSpec(memory_space=pl.ANY),
            pl.BlockSpec(memory_space=pltpu.VMEM),
            pl.BlockSpec(memory_space=pltpu.VMEM),
            pl.BlockSpec(memory_space=pl.ANY),
        ],
        out_specs=pl.BlockSpec(memory_space=pl.ANY),
        scratch_shapes=[
            pltpu.VMEM((lats + 2 * WIDTH,) + tall, kept.dtype),
            pltpu.VMEM((lats, lanes, 2 * width), kept.dtype),
            pltpu.VMEM(row_coefs.shape, kept.dtype),
            pltpu.VMEM((3,) + tall, kept.dtype),
            pltpu.VMEM((3,) + tall, kept.dtype),
            pltpu.VMEM((2 * WIDTH, lanes, lanes), kept.dtype),
            pltpu.SemaphoreType.DMA((2, parts)),
            pltpu.SemaphoreType.DMA,
            pltpu.SemaphoreType.DMA((2, parts)),
            pltpu.SemaphoreType.DMA((2, parts)),
            pltpu.SemaphoreType.DMA,
        ],
        input_output_aliases={1 + count + 5: 0},
        compiler_params=pltpu.CompilerParams(vmem_limit_bytes=VMEM_LIMIT),
        cost_estimate=pl.CostEstimate(
            flops=26 * rows * cols, bytes_accessed=20 * rows * width, transcendentals=0
        ),
        name="rim",
    )(slots, *got, low, high, row_coefs, col_coefs, mixers, kept)
    return result.reshape(rows, cols)


def coefficients(velocity_x, velocity_y, diffusion, start, count, reach):
    stack = jnp.stack(
        [
            diffusion - 0.5 * velocity_x,
            diffusion + 0.5 * velocity_x,
            diffusion - 0.5 * velocity_y,
            diffusion + 0.5 * velocity_y,
            -4.0 * diffusion,
        ],
        axis=1,
    )
    padded = jnp.pad(stack, ((reach, reach), (0, 0), (0, 0)))
    return lax.dynamic_slice_in_dim(padded, start, count + 2 * reach, 0)


def circulants(coefs):
    lanes = coefs.shape[-1]
    source = lax.broadcasted_iota(jnp.int32, (lanes, lanes), 0)
    target = lax.broadcasted_iota(jnp.int32, (lanes, lanes), 1)
    apart = jnp.mod(source - target, lanes)
    east, west, here = (coefs[:, k, None, :] for k in (0, 1, 4))
    matrix = jnp.where(apart == 1, east, 0.0) + jnp.where(apart == lanes - 1, west, 0.0)
    matrix = matrix + jnp.where(apart == 0, here, 0.0)
    coarse = lax.reduce_precision(matrix, 8, 7)
    both = jnp.concatenate([coarse, matrix - coarse], axis=2).astype(jnp.bfloat16)
    return jnp.concatenate([both, both], axis=1)


def solution(mesh):
    rows, cols = mesh.shape["row"], mesh.shape["col"]

    def shards(cov, noise, velocity_x, velocity_y, diffusion):
        lanes = velocity_x.shape[1]
        tile_rows, tile_cols = cov.shape
        lat_row, lat_col = tile_rows // lanes, tile_cols // lanes
        chosen, piece, parts = halo_plan(rows, cols, lat_row, lat_col)
        edges = [(source, target) for source, target, *_ in chosen]
        rounds, order = colour(edges)
        send = [[[0, 0, 0] for _ in range(rounds)] for _ in range(rows * cols)]
        slots = [[-1] * (2 * parts) for _ in range(rows * cols)]
        pairs = [[] for _ in range(rounds)]
        for (source, target, (side, part), where, _), n in zip(chosen, order):
            flat_source = source[0] * cols + source[1]
            flat_target = target[0] * cols + target[1]
            send[flat_source][n] = list(where)
            slots[flat_target][side * parts + part] = n
            pairs[n].append((flat_source, flat_target))
        row, col = lax.axis_index("row"), lax.axis_index("col")
        here = row * cols + col
        send = lax.dynamic_index_in_dim(jnp.array(send, jnp.int32), here, 0, False)
        slots = lax.dynamic_index_in_dim(jnp.array(slots, jnp.int32), here, 0, False)

        up = [(r, r + 1) for r in range(rows - 1)]
        down = [(b, a) for a, b in up]
        reach = WIDTH * lanes
        top, bottom, send = lax.optimization_barrier(
            (cov[tile_rows - reach :], cov[:reach], send)
        )
        low = lax.ppermute(top, "row", up)
        high = lax.ppermute(bottom, "row", down)
        packed = [pack(send[n], cov, piece, lanes) for n in range(rounds)]
        got = [lax.ppermute(v, ("row", "col"), p) for v, p in zip(packed, pairs)]

        narrow = coefficients(
            velocity_x, velocity_y, diffusion, row * lat_row, lat_row, WIDTH
        )
        row_coefs = jnp.broadcast_to(narrow[..., None], narrow.shape + (lanes,))
        col_coefs = coefficients(velocity_x, velocity_y, diffusion, col * lat_col, lat_col, 2)
        mixers = circulants(col_coefs)
        forecast = stream(Inner(lat_row), (cov,), noise, row_coefs, col_coefs, mixers, lanes)
        low, high, forecast = lax.optimization_barrier((low, high, forecast))
        forecast = stream(
            Ends(lat_row), (low, cov, high), noise, row_coefs, col_coefs, mixers, lanes, forecast
        )
        forecast, *got = lax.optimization_barrier((forecast, *got))

        first, last = corners(slots, got, parts)
        low = lax.ppermute(last, "row", up)
        high = lax.ppermute(first, "row", down)
        return rim(
            slots, got, low, high, row_coefs, col_coefs, mixers, forecast, parts, lanes
        )

    spec = P("row", "col")
    return jax.shard_map(
        shards,
        mesh=mesh,
        in_specs=(spec, spec, P(), P(), P()),
        out_specs=spec,
        check_vma=False,
    )
```

```python
import functools
import random

import jax
import jax.numpy as jnp
from jax import lax
from jax.experimental import pallas as pl
from jax.experimental.pallas import tpu as pltpu
from jax.sharding import PartitionSpec as P

VMEM_LIMIT = 62 * 1024 * 1024
SUBLANES = 8
COL_ROWS = 128
third = 1.0 / 3.0


WIDTH = 3


def route(source, target):
    (sr, sc, xs), (tr, tc, _) = source, target
    steps = []
    here = [sc // xs, sc % xs, sr // 2]
    goal = [tc // xs, tc % xs, tr // 2]
    for axis in range(3):
        while here[axis] != goal[axis]:
            step = 1 if goal[axis] > here[axis] else -1
            steps.append((tuple(here), axis, step))
            here[axis] += step
    return steps


def halo_plan(rows, cols, lat_row, lat_col):
    xs = max(cols // 4, 1)
    piece = min(lat_row, lat_col)
    parts = lat_row // piece
    wants = []
    for r in range(rows):
        for c in range(cols):
            for side in range(2):
                near = c - 1 + 2 * side
                if not 0 <= near < cols:
                    continue
                lat_j = c * lat_col - WIDTH if side == 0 else (c + 1) * lat_col
                for part in range(parts):
                    lat_i = r * lat_row + part * piece
                    direct = ((r, near), (0, part * piece, lat_j % lat_col))
                    mirror = (
                        (lat_j // lat_row, lat_i // lat_col),
                        (1, lat_j % lat_row, lat_i % lat_col),
                    )
                    options = []
                    for (sr, sc), where in (direct, mirror):
                        links = route((sr, sc, xs), (r, c, xs))
                        away = (sr, sc) != (r, c)
                        options.append(((sr, sc), where, links, (side, away)))
                    wants.append(((r, c), (side, part), options))
    load, part_load = {}, {}
    for r in range(rows - 1):
        for c in range(cols):
            for a, b in (((r, c, xs), (r + 1, c, xs)), ((r + 1, c, xs), (r, c, xs))):
                for link in route(a, b):
                    load[link] = load.get(link, 0) + 1
    degree = {}
    limit = parts

    rng = random.Random(0)
    pick = [0] * len(wants)

    def put(option, sign):
        source, _, links, (side, away) = option
        for link in links:
            load[link] = load.get(link, 0) + sign
            part_load[side, link] = part_load.get((side, link), 0) + sign
        if away:
            degree[source, side] = degree.get((source, side), 0) + sign

    def price(option, weight):
        source, _, links, (side, away) = option
        cost = 0
        for link in links:
            n, m = load.get(link, 0), part_load.get((side, link), 0)
            cost += (n + 1) ** 6 - n**6 + (m + 1) ** 6 - m**6
        over = max(degree.get((source, side), 0) + 1 - limit, 0) if away else 0
        return cost + weight * over

    def score():
        over = sum(max(n - limit, 0) for n in degree.values())
        return over, sum(n**6 for n in load.values()) + sum(
            n**6 for n in part_load.values()
        )

    for _, _, options in wants:
        put(options[0], 1)
    best, kept = score(), list(pick)
    for sweep in range(64000 // (rows * cols)):
        heat = 1.0 - (sweep % 100) / 100
        order = list(range(len(wants)))
        rng.shuffle(order)
        for n in order:
            options = wants[n][2]
            put(options[pick[n]], -1)
            costs = [price(o, 20000.0) + 20000.0 * heat * rng.random() for o in options]
            pick[n] = costs.index(min(costs))
            put(options[pick[n]], 1)
        now = score()
        if now < best:
            best, kept = now, list(pick)
    chosen = []
    for n, (target, slot, options) in enumerate(wants):
        source, where, links, _ = options[kept[n]]
        chosen.append((source, target, slot, where, links))
    return chosen, piece, parts


def colour(edges):
    at_source, at_target, result = {}, {}, {}
    degree = {}
    for source, target in edges:
        degree[("s", source)] = degree.get(("s", source), 0) + 1
        degree[("t", target)] = degree.get(("t", target), 0) + 1
    rounds = max(degree.values())
    for n, (source, target) in enumerate(edges):
        used_s = at_source.setdefault(source, {})
        used_t = at_target.setdefault(target, {})
        a = next(k for k in range(rounds) if k not in used_s)
        b = next(k for k in range(rounds) if k not in used_t)
        if a != b:
            chain, side, node, want = [], "t", target, a
            while True:
                table = at_target[node] if side == "t" else at_source[node]
                if want not in table:
                    break
                edge = table[want]
                chain.append(edge)
                node = edges[edge][0] if side == "t" else edges[edge][1]
                side = "s" if side == "t" else "t"
                want = b if want == a else a
            for edge in chain:
                s, t = edges[edge]
                del at_source[s][result[edge]], at_target[t][result[edge]]
            for edge in chain:
                s, t = edges[edge]
                result[edge] = b if result[edge] == a else a
                at_source[s][result[edge]] = edge
                at_target[t][result[edge]] = edge
        result[n] = a
        used_s[a] = n
        used_t[a] = n
    return rounds, [result[n] for n in range(len(edges))]


def pack_kernel(count, parts, lanes, step_lats, where, cov, *refs):
    outs, (straight, turned, in_sems, out_sems) = refs[:count], refs[count:]
    width = WIDTH * lanes
    span = step_lats * lanes

    def facts(p):
        row = pl.multiple_of(where[4 * p + 2] * lanes, lanes)
        col = pl.multiple_of(where[4 * p + 3] * lanes, lanes)
        used, flip = where[4 * p] == 1, where[4 * p + 1] == 1
        return used, used & flip, used & ~flip, row, col

    def copies(p, n, row, col):
        band = pl.ds(n * span, span)
        return (
            pltpu.make_async_copy(
                cov.at[pl.ds(row + n * span, span), pl.ds(col, width)],
                straight.at[p, band, :],
                in_sems.at[p, n],
            ),
            pltpu.make_async_copy(
                cov.at[pl.ds(row, width), pl.ds(col + n * span, span)],
                turned.at[p, :, band],
                in_sems.at[p, n],
            ),
            pltpu.make_async_copy(straight.at[p, band, :], outs[p].at[band, :], out_sems.at[p, n]),
        )

    for p in range(count):
        used, flipped, plain, row, col = facts(p)
        for n in range(parts):
            direct, mirror, _ = copies(p, n, row, col)
            pl.when(plain)(direct.start)
            pl.when(flipped)(mirror.start)
    for p in range(count):
        used, flipped, plain, row, col = facts(p)
        for n in range(parts):
            direct, mirror, leave = copies(p, n, row, col)
            pl.when(plain)(direct.wait)

            @pl.when(flipped)
            def _():
                mirror.wait()
                for a in range(step_lats):
                    lat = n * step_lats + a
                    rows = slice(lat * lanes, (lat + 1) * lanes)
                    for b in range(WIDTH):
                        cols = slice(b * lanes, (b + 1) * lanes)
                        straight[p, rows, cols] = turned[p, cols, rows].T

            pl.when(used)(leave.start)
    for p in range(count):
        used, flipped, plain, row, col = facts(p)
        for n in range(parts):
            pl.when(used)(copies(p, n, row, col)[2].wait)


def pack(where, cov, count, piece, lanes):
    parts = max(piece // 4, 1)
    step = piece // parts
    tall, width = piece * lanes, WIDTH * lanes
    shape = jax.ShapeDtypeStruct((tall, width), cov.dtype)
    return pl.pallas_call(
        functools.partial(pack_kernel, count, parts, lanes, step),
        out_shape=(shape,) * count,
        in_specs=[
            pl.BlockSpec(memory_space=pltpu.SMEM),
            pl.BlockSpec(memory_space=pl.ANY),
        ],
        out_specs=(pl.BlockSpec(memory_space=pl.ANY),) * count,
        scratch_shapes=[
            pltpu.VMEM((count, tall, width), cov.dtype),
            pltpu.VMEM((count, width, tall), cov.dtype),
            pltpu.SemaphoreType.DMA((count, parts)),
            pltpu.SemaphoreType.DMA((count, parts)),
        ],
        compiler_params=pltpu.CompilerParams(vmem_limit_bytes=VMEM_LIMIT),
        cost_estimate=pl.CostEstimate(
            flops=0, bytes_accessed=8 * count * tall * width, transcendentals=0
        ),
        name="pack",
    )(where, cov)


def row_step(strips, fields, slots, lats, row_coefs, half):
    source, one, two = fields
    (c0, c1, c2, c3), (f1, f2, f3), (g1, g2, g3) = slots
    lanes = half.shape[1]
    tiles = lanes // SUBLANES
    place = lax.broadcasted_iota(jnp.int32, (SUBLANES, half.shape[2]), 0)
    top, bottom = place == SUBLANES - 1, place == 0

    @pl.loop(0, strips)
    def _(s):
        def tile(field, slot, r):
            return field[slot, s, r * SUBLANES : (r + 1) * SUBLANES, :]

        def turns(field, slot, r):
            here = tile(field, slot, r)
            return here, pltpu.roll(here, SUBLANES - 1, 0), pltpu.roll(here, 1, 0)

        def weigh(stage, r, around, north, south):
            last, (here, up, down), following = around
            coefs = [
                row_coefs[stage][lats[stage], k, r * SUBLANES : (r + 1) * SUBLANES, :] for k in range(5)
            ]
            east = jnp.where(top, following[1], up)
            west = jnp.where(bottom, last[2], down)
            return (
                coefs[0] * east
                + coefs[1] * west
                + coefs[2] * north
                + coefs[3] * south
                + coefs[4] * here
            )

        rolled = [(source, c1), (one, f2), (two, g2)]
        start = [[turns(*f, tiles - 1), turns(*f, 0)] for f in rolled]
        around = [list(w) for w in start]
        for r in range(tiles):
            span = slice(r * SUBLANES, (r + 1) * SUBLANES)
            for n, f in enumerate(rolled):
                around[n].append(start[n][1] if r + 1 == tiles else turns(*f, r + 1))
            mid = tile(source, c2, r)
            v1 = around[0][1][0] + third * weigh(0, r, around[0], tile(source, c0, r), mid)
            v2 = mid + 0.5 * weigh(1, r, around[1], v1, tile(one, f3, r))
            half[s, span, :] = tile(source, c3, r) + weigh(
                2, r, around[2], v2, tile(two, g3, r)
            )
            one[f1, s, span, :] = v1
            two[g1, s, span, :] = v2
            for w in around:
                del w[0]


def ring_slots(step):
    field = [lax.rem(step + 4 - back, 4) for back in range(4)]
    one = [lax.rem(step + 6 - back, 3) for back in range(3)]
    return field, one, one


def col_stage(fields, lat, weights, mixers):
    total = None
    if lat in fields:
        here = fields[lat]
        lanes = here.shape[1]
        coarse = here.astype(jnp.bfloat16)
        fine = (here - coarse.astype(jnp.float32)).astype(jnp.bfloat16)
        both = jnp.dot(
            jnp.concatenate([coarse, fine], axis=1),
            mixers[lat + 2],
            preferred_element_type=jnp.float32,
        )
        total = both[:, :lanes] + both[:, lanes:]
    for step, k in ((1, 2), (-1, 3)):
        if lat + step in fields:
            value = weights[lat + 2, k : k + 1, :] * fields[lat + step]
            total = value if total is None else total + value
    return total


def plus(fields, lat, value):
    return fields[lat] + value if lat in fields else value


def stream_kernel(plan, lat_col, lanes, *refs):
    sources = refs[: plan.sources]
    noise, *row_coefs, col_coefs, mixers = refs[plan.sources : plan.sources + 6]
    out, ring, one, two, half, first, second = refs[-7:]
    step = pl.program_id(0)
    local = plan.local(step)
    slots = ring_slots(step)

    for source, when in zip(sources, plan.which(step)):

        @pl.when(when)
        def _():
            slot = slots[0][0]
            for s in range(lat_col):
                ring[slot, s] = source[:, s * lanes : (s + 1) * lanes]

    @pl.when(local >= 2)
    def _():
        row_step(lat_col, (ring, one, two), slots, [0, 0, 0], row_coefs, half)

    @pl.when(local >= 2 * WIDTH)
    def _():
        @pl.loop(0, lanes // COL_ROWS)
        def _(n):
            rows = pl.ds(pl.multiple_of(n * COL_ROWS, COL_ROWS), COL_ROWS)
            u = Stored(half, rows, 0, range(lat_col))
            v = Stored(first, rows, 1, [])
            w = Stored(second, rows, 1, [])
            for lat in range(-1, lat_col + 3):
                if lat <= lat_col:
                    v[lat] = plus(u, lat, third * col_stage(u, lat, col_coefs, mixers))
                at = lat - 1
                if -1 <= at <= lat_col:
                    w[at] = plus(u, at, 0.5 * col_stage(v, at, col_coefs, mixers))
                at = lat - 2
                if 0 <= at < lat_col:
                    span = slice(at * lanes, (at + 1) * lanes)
                    value = u[at] + col_stage(w, at, col_coefs, mixers)
                    out[rows, span] = value + noise[rows, span]


class Stored:
    def __init__(self, ref, rows, shift, lats):
        self.ref, self.rows, self.shift, self.lats = ref, rows, shift, set(lats)

    def __contains__(self, lat):
        return lat in self.lats

    def __getitem__(self, lat):
        return self.ref[lat + self.shift, self.rows, :]

    def __setitem__(self, lat, value):
        self.lats.add(lat)
        self.ref[lat + self.shift, self.rows, :] = value


class Inner:
    sources = 1

    def __init__(self, lats):
        self.lats = lats
        self.steps = lats

    def local(self, step):
        return step

    def lat(self, step):
        return step

    def which(self, step):
        return (step >= 0,)

    def inputs(self):
        return (lambda n: (n, 0),)

    def output(self, step):
        return (jnp.clip(step - WIDTH, WIDTH, self.lats - WIDTH - 1), 0)


class Ends:
    sources = 3

    def __init__(self, lats):
        self.lats = lats
        self.steps = 6 * WIDTH

    def local(self, step):
        return lax.rem(step, 3 * WIDTH)

    def lat(self, step):
        upper = step >= 3 * WIDTH
        return jnp.where(upper, self.lats - 5 * WIDTH + step, step - WIDTH)

    def which(self, step):
        lat = self.lat(step)
        return lat < 0, (lat >= 0) & (lat < self.lats), lat >= self.lats

    def inputs(self):
        def low(n):
            return (jnp.minimum(n, WIDTH - 1), 0)

        def own(n):
            return (jnp.clip(self.lat(n), 0, self.lats - 1), 0)

        def high(n):
            return (jnp.clip(self.lat(n) - self.lats, 0, WIDTH - 1), 0)

        return low, own, high

    def output(self, step):
        upper = step >= 3 * WIDTH
        back = jnp.maximum(self.local(step) - 2 * WIDTH, 0)
        return (jnp.where(upper, self.lats - WIDTH, 0) + back, 0)


def stream(plan, sources, noise, row_coefs, col_coefs, mixers, lanes, kept=None):
    rows, cols = noise.shape
    lat_col = cols // lanes
    band = (lanes, cols)
    tall = (lat_col, lanes, lanes)

    def coef_spec(back):
        def index(n):
            return (jnp.maximum(plan.lat(n) + WIDTH - back, 0), 0, 0, 0)

        return pl.BlockSpec((1,) + row_coefs.shape[1:], index)

    extra, aliases = (), {}
    extra_specs = []
    if kept is not None:
        extra = (kept,)
        extra_specs = [pl.BlockSpec(memory_space=pl.ANY)]
        aliases = {plan.sources + 6: 0}
    work = rows * cols * plan.steps // (rows // lanes)
    return pl.pallas_call(
        functools.partial(stream_kernel, plan, lat_col, lanes),
        grid=(plan.steps,),
        out_shape=jax.ShapeDtypeStruct(noise.shape, noise.dtype),
        in_specs=[pl.BlockSpec(band, index) for index in plan.inputs()]
        + [
            pl.BlockSpec(band, plan.output),
        ]
        + [coef_spec(back) for back in (1, 2, 3)]
        + [
            pl.BlockSpec(memory_space=pltpu.VMEM),
            pl.BlockSpec(memory_space=pltpu.VMEM),
        ]
        + extra_specs,
        out_specs=pl.BlockSpec(band, plan.output),
        scratch_shapes=[
            pltpu.VMEM((4,) + tall, noise.dtype),
            pltpu.VMEM((3,) + tall, noise.dtype),
            pltpu.VMEM((3,) + tall, noise.dtype),
            pltpu.VMEM((lat_col, lanes, lanes), noise.dtype),
            pltpu.VMEM((lat_col + 2, lanes, lanes), noise.dtype),
            pltpu.VMEM((lat_col + 2, lanes, lanes), noise.dtype),
        ],
        input_output_aliases=aliases,
        compiler_params=pltpu.CompilerParams(
            vmem_limit_bytes=VMEM_LIMIT, dimension_semantics=("arbitrary",)
        ),
        cost_estimate=pl.CostEstimate(
            flops=70 * work, bytes_accessed=12 * work, transcendentals=0
        ),
        name=type(plan).__name__.lower(),
    )(*sources, noise, row_coefs, row_coefs, row_coefs, col_coefs, mixers, *extra)


def corner_kernel(count, parts, slots, *refs):
    got, (first, last, sems) = (refs[:count], refs[count : 2 * count]), refs[2 * count :]
    piece, _, width = got[0][0].shape
    ends = ((0, first, 0), (parts - 1, last, piece - WIDTH))
    for go in (0, 1):
        for side in range(2):
            for k, (part, ref, lat) in enumerate(ends):
                slot = slots[side * parts + part]
                target = ref.at[:, :, pl.ds(side * width, width)]
                for n in range(count):

                    @pl.when(slot == n)
                    def _():
                        copy = pltpu.make_async_copy(
                            got[side][n].at[pl.ds(lat, WIDTH)], target, sems.at[side, k]
                        )
                        copy.wait() if go else copy.start()

                if not go:

                    @pl.when(slot < 0)
                    def _():
                        target[...] = jnp.zeros(target.shape, target.dtype)


def corners(slots, got, parts):
    _, lanes, width = got[0].shape
    shape = jax.ShapeDtypeStruct((WIDTH, lanes, 2 * width), got[0].dtype)
    return pl.pallas_call(
        functools.partial(corner_kernel, len(got) // 2, parts),
        out_shape=(shape, shape),
        in_specs=[pl.BlockSpec(memory_space=pltpu.SMEM)]
        + [pl.BlockSpec(memory_space=pl.ANY)] * len(got),
        out_specs=(pl.BlockSpec(memory_space=pltpu.VMEM),) * 2,
        scratch_shapes=[pltpu.SemaphoreType.DMA((2, 2))],
        compiler_params=pltpu.CompilerParams(vmem_limit_bytes=VMEM_LIMIT),
        name="corners",
    )(slots, *got)


def rim_kernel(count, parts, lats, lat_col, lanes, slots, *refs):
    got = refs[:count], refs[count : 2 * count]
    low, high, row_coefs_hbm, col_coefs, mixers, _, out = refs[2 * count : 2 * count + 7]
    (halo, edge, row_coefs, one, two, half, got_sem, end_sem, in_sem, out_sem, coef_sem) = refs[
        2 * count + 7 :
    ]
    piece = lats // parts
    width = WIDTH * lanes
    tall = lats + 2 * WIDTH
    bounds = [0] + [WIDTH + (p + 1) * piece for p in range(parts - 1)] + [tall]

    def strip_of(field, strip):
        return field.at[:, :, pl.ds(strip * lanes, lanes)]

    def place(first, depth, strip):
        return halo.at[pl.ds(first, depth), strip]

    def end_copies():
        for n in range(2 * WIDTH):
            yield pltpu.make_async_copy(strip_of(low, n), place(0, WIDTH, n), end_sem)
            yield pltpu.make_async_copy(strip_of(high, n), place(WIDTH + lats, WIDTH, n), end_sem)

    def coef_copy(part):
        span = pl.ds(bounds[part], bounds[part + 1] - bounds[part])
        return pltpu.make_async_copy(row_coefs_hbm.at[span], row_coefs.at[span], coef_sem.at[part])

    def each_piece(part, go):
        first = WIDTH + part * piece
        for side in range(2):
            slot = slots[side * parts + part]
            for n in range(count):

                @pl.when(slot == n)
                def _():
                    for k in range(WIDTH):
                        copy = pltpu.make_async_copy(
                            strip_of(got[side][n], k),
                            place(first, piece, side * WIDTH + k),
                            got_sem.at[side, part],
                        )
                        copy.wait() if go else copy.start()

            if not go:

                @pl.when(slot < 0)
                def _():
                    @pl.loop(first, first + piece)
                    def _(lat):
                        halo[lat, side * WIDTH : (side + 1) * WIDTH] = jnp.zeros(
                            (WIDTH, lanes, lanes), halo.dtype
                        )

    def edge_copy(part, side, inward):
        outside = out.at[
            pl.ds(part * piece, piece), :, pl.ds(side * (lat_col - WIDTH) * lanes, width)
        ]
        inside = edge.at[pl.ds(part * piece, piece), :, pl.ds(side * width, width)]
        if inward:
            return pltpu.make_async_copy(outside, inside, in_sem.at[side, part])
        return pltpu.make_async_copy(inside, outside, out_sem.at[side, part])

    for copy in end_copies():
        copy.start()
    for part in range(parts):
        each_piece(part, False)
        coef_copy(part).start()
        for side in range(2):
            edge_copy(part, side, True).start()
    for copy in end_copies():
        copy.wait()

    def one_lat(step):
        _, early, later = ring_slots(step)

        @pl.when(step >= 2)
        def _():
            back = [jnp.maximum(step - n, 0) for n in range(4)]
            row_step(
                2 * WIDTH, (halo, one, two), (back, early, later), back[1:], [row_coefs] * 3, half
            )

        @pl.when(step >= 2 * WIDTH)
        def _():
            lat = step - 2 * WIDTH
            for side in range(2):
                def at(d):
                    return d if side == 0 else lat_col - 1 - d

                base = side * WIDTH
                u = {at(d): half[base + (d + WIDTH if side == 0 else -d - 1)] for d in (-3, -2, -1)}
                v = {
                    at(d): plus(u, at(d), third * col_stage(u, at(d), col_coefs, mixers))
                    for d in (-2, -1, 0)
                }
                w = {
                    at(d): plus(u, at(d), 0.5 * col_stage(v, at(d), col_coefs, mixers))
                    for d in (-1, 0, 1)
                }
                for d in range(WIDTH):
                    start = side * width + (d if side == 0 else WIDTH - 1 - d) * lanes
                    span = slice(start, start + lanes)
                    value = col_stage(w, at(d), col_coefs, mixers)
                    edge[lat, :, span] = edge[lat, :, span] + value

    for part in range(parts):
        each_piece(part, True)
        coef_copy(part).wait()
        for side in range(2):
            edge_copy(part, side, True).wait()

        @pl.loop(bounds[part], bounds[part + 1])
        def _(step):
            one_lat(step)

        if part > 0:
            for side in range(2):
                edge_copy(part - 1, side, False).start()
    for side in range(2):
        edge_copy(parts - 1, side, False).start()
    for part in range(parts):
        for side in range(2):
            edge_copy(part, side, False).wait()


def rim(slots, got, low, high, row_coefs, col_coefs, mixers, forecast, parts, lanes):
    rows, cols = forecast.shape
    lats, lat_col = rows // lanes, cols // lanes
    count = len(got) // 2
    width = WIDTH * lanes
    kept = forecast.reshape(lats, lanes, cols)
    tall = (2 * WIDTH, lanes, lanes)
    anywhere = pl.BlockSpec(memory_space=pl.ANY)
    vmem = pl.BlockSpec(memory_space=pltpu.VMEM)
    result = pl.pallas_call(
        functools.partial(rim_kernel, count, parts, lats, lat_col, lanes),
        out_shape=jax.ShapeDtypeStruct(kept.shape, kept.dtype),
        in_specs=[pl.BlockSpec(memory_space=pltpu.SMEM)]
        + [anywhere] * (2 * count + 3)
        + [vmem, vmem, anywhere],
        out_specs=anywhere,
        scratch_shapes=[
            pltpu.VMEM((lats + 2 * WIDTH,) + tall, kept.dtype),
            pltpu.VMEM((lats, lanes, 2 * width), kept.dtype),
            pltpu.VMEM(row_coefs.shape, kept.dtype),
            pltpu.VMEM((3,) + tall, kept.dtype),
            pltpu.VMEM((3,) + tall, kept.dtype),
            pltpu.VMEM(tall, kept.dtype),
            pltpu.SemaphoreType.DMA((2, parts)),
            pltpu.SemaphoreType.DMA,
            pltpu.SemaphoreType.DMA((2, parts)),
            pltpu.SemaphoreType.DMA((2, parts)),
            pltpu.SemaphoreType.DMA((parts,)),
        ],
        input_output_aliases={1 + 2 * count + 5: 0},
        compiler_params=pltpu.CompilerParams(vmem_limit_bytes=VMEM_LIMIT),
        cost_estimate=pl.CostEstimate(
            flops=13 * rows * cols, bytes_accessed=20 * rows * width, transcendentals=0
        ),
        name="rim",
    )(slots, *got, low, high, row_coefs, col_coefs, mixers, kept)
    return result.reshape(rows, cols)


def coefficients(velocity_x, velocity_y, diffusion, start, count, reach):
    stack = jnp.stack(
        [
            diffusion - 0.5 * velocity_x,
            diffusion + 0.5 * velocity_x,
            diffusion - 0.5 * velocity_y,
            diffusion + 0.5 * velocity_y,
            -4.0 * diffusion,
        ],
        axis=1,
    )
    padded = jnp.pad(stack, ((reach, reach), (0, 0), (0, 0)))
    return lax.dynamic_slice_in_dim(padded, start, count + 2 * reach, 0)


def circulants(coefs):
    lanes = coefs.shape[-1]
    source = lax.broadcasted_iota(jnp.int32, (lanes, lanes), 0)
    target = lax.broadcasted_iota(jnp.int32, (lanes, lanes), 1)
    apart = jnp.mod(source - target, lanes)
    east, west, here = (coefs[:, k, None, :] for k in (0, 1, 4))
    matrix = jnp.where(apart == 1, east, 0.0) + jnp.where(apart == lanes - 1, west, 0.0)
    matrix = matrix + jnp.where(apart == 0, here, 0.0)
    coarse = lax.reduce_precision(matrix, 8, 7)
    both = jnp.concatenate([coarse, matrix - coarse], axis=2).astype(jnp.bfloat16)
    return jnp.concatenate([both, both], axis=1)


def solution(mesh):
    rows, cols = mesh.shape["row"], mesh.shape["col"]

    def shards(cov, noise, velocity_x, velocity_y, diffusion):
        lanes = velocity_x.shape[1]
        tile_rows, tile_cols = cov.shape
        lat_row, lat_col = tile_rows // lanes, tile_cols // lanes
        chosen, piece, parts = halo_plan(rows, cols, lat_row, lat_col)
        row, col = lax.axis_index("row"), lax.axis_index("col")
        here = row * cols + col

        def flat(place):
            return place[0] * cols + place[1]

        def mine(table):
            return lax.dynamic_index_in_dim(jnp.array(table, jnp.int32), here, 0, False)

        sides = []
        for side in range(2):
            jobs = [job for job in chosen if job[2][0] == side]
            away = [job for job in jobs if job[0] != job[1]]
            rounds, order = colour([(job[0], job[1]) for job in away])
            order = order + [rounds] * (len(jobs) - len(away))
            send = [[0] * (4 * (rounds + 1)) for _ in range(rows * cols)]
            slots = [[-1] * parts for _ in range(rows * cols)]
            pairs = [[] for _ in range(rounds)]
            for job, n in zip(away + [job for job in jobs if job[0] == job[1]], order):
                source, target, (_, part), where, _ = job
                send[flat(source)][4 * n : 4 * n + 4] = [1, *where]
                slots[flat(target)][part] = n
                if n < rounds:
                    pairs[n].append((flat(source), flat(target)))
            sides.append((rounds, mine(send), mine(slots), pairs))

        up = [(r, r + 1) for r in range(rows - 1)]
        down = [(b, a) for a, b in up]
        reach = WIDTH * lanes
        top, bottom = cov[tile_rows - reach :], cov[:reach]
        low = lax.ppermute(top, "row", up)
        high = lax.ppermute(bottom, "row", down)
        got = []
        ahead = (top, bottom)
        for rounds, send, _, pairs in sides:
            send, *ahead = lax.optimization_barrier((send, *ahead))
            packed = pack(send, cov, rounds + 1, piece, lanes)
            ahead = [packed[-1]]
            moved = [lax.ppermute(v, ("row", "col"), p) for v, p in zip(packed, pairs)]
            got.append([v.reshape(piece, lanes, reach) for v in [*moved, packed[-1]]])

        narrow = coefficients(
            velocity_x, velocity_y, diffusion, row * lat_row, lat_row, WIDTH
        )
        row_coefs = jnp.broadcast_to(narrow[..., None], narrow.shape + (lanes,))
        col_coefs = coefficients(velocity_x, velocity_y, diffusion, col * lat_col, lat_col, 2)
        mixers = circulants(col_coefs)
        forecast = stream(Inner(lat_row), (cov,), noise, row_coefs, col_coefs, mixers, lanes)
        low, high, forecast = lax.optimization_barrier((low, high, forecast))
        forecast = stream(
            Ends(lat_row), (low, cov, high), noise, row_coefs, col_coefs, mixers, lanes, forecast
        )
        most = max(len(buffers) for buffers in got)
        got = [[*buffers, *[buffers[-1]] * (most - len(buffers))] for buffers in got]
        forecast, *pieces = lax.optimization_barrier((forecast, *got[0], *got[1]))
        slots = jnp.concatenate([slots for _, _, slots, _ in sides])
        first, last = corners(slots, pieces, parts)
        low = lax.ppermute(last, "row", up)
        high = lax.ppermute(first, "row", down)
        forecast = rim(
            slots, pieces, low, high, row_coefs, col_coefs, mixers, forecast, parts, lanes
        )
        return forecast

    spec = P("row", "col")
    return jax.shard_map(
        shards,
        mesh=mesh,
        in_specs=(spec, spec, P(), P(), P()),
        out_specs=spec,
        check_vma=False,
    )
```

```python
import functools
import random

import jax
import jax.numpy as jnp
from jax import lax
from jax.experimental import pallas as pl
from jax.experimental.pallas import tpu as pltpu
from jax.sharding import PartitionSpec as P

VMEM_LIMIT = 62 * 1024 * 1024
SUBLANES = 8
COL_ROWS = 128
third = 1.0 / 3.0


WIDTH = 3


def route(source, target):
    (sr, sc, xs), (tr, tc, _) = source, target
    steps = []
    here = [sc // xs, sc % xs, sr // 2]
    goal = [tc // xs, tc % xs, tr // 2]
    for axis in range(3):
        while here[axis] != goal[axis]:
            step = 1 if goal[axis] > here[axis] else -1
            steps.append((tuple(here), axis, step))
            here[axis] += step
    return steps


def halo_plan(rows, cols, lat_row, lat_col):
    xs = max(cols // 4, 1)
    piece = min(lat_row, lat_col)
    parts = lat_row // piece
    wants = []
    for r in range(rows):
        for c in range(cols):
            for side in range(2):
                near = c - 1 + 2 * side
                if not 0 <= near < cols:
                    continue
                lat_j = c * lat_col - WIDTH if side == 0 else (c + 1) * lat_col
                for part in range(parts):
                    lat_i = r * lat_row + part * piece
                    direct = ((r, near), (0, part * piece, lat_j % lat_col))
                    mirror = (
                        (lat_j // lat_row, lat_i // lat_col),
                        (1, lat_j % lat_row, lat_i % lat_col),
                    )
                    options = []
                    for (sr, sc), where in (direct, mirror):
                        links = route((sr, sc, xs), (r, c, xs))
                        away = (sr, sc) != (r, c)
                        options.append(((sr, sc), where, links, (side, away)))
                    wants.append(((r, c), (side, part), options))
    load, part_load = {}, {}
    for r in range(rows - 1):
        for c in range(cols):
            for a, b in (((r, c, xs), (r + 1, c, xs)), ((r + 1, c, xs), (r, c, xs))):
                for link in route(a, b):
                    load[link] = load.get(link, 0) + 1
    degree = {}
    limit = parts

    rng = random.Random(0)
    pick = [0] * len(wants)

    def put(option, sign):
        source, _, links, (side, away) = option
        for link in links:
            load[link] = load.get(link, 0) + sign
            part_load[side, link] = part_load.get((side, link), 0) + sign
        if away:
            degree[source, side] = degree.get((source, side), 0) + sign

    def price(option, weight):
        source, _, links, (side, away) = option
        cost = 0
        for link in links:
            n, m = load.get(link, 0), part_load.get((side, link), 0)
            cost += (n + 1) ** 6 - n**6 + (m + 1) ** 6 - m**6
        over = max(degree.get((source, side), 0) + 1 - limit, 0) if away else 0
        return cost + weight * over

    def score():
        over = sum(max(n - limit, 0) for n in degree.values())
        return over, sum(n**6 for n in load.values()) + sum(
            n**6 for n in part_load.values()
        )

    for _, _, options in wants:
        put(options[0], 1)
    best, kept = score(), list(pick)
    for sweep in range(64000 // (rows * cols)):
        heat = 1.0 - (sweep % 100) / 100
        order = list(range(len(wants)))
        rng.shuffle(order)
        for n in order:
            options = wants[n][2]
            put(options[pick[n]], -1)
            costs = [price(o, 20000.0) + 20000.0 * heat * rng.random() for o in options]
            pick[n] = costs.index(min(costs))
            put(options[pick[n]], 1)
        now = score()
        if now < best:
            best, kept = now, list(pick)
    chosen = []
    for n, (target, slot, options) in enumerate(wants):
        source, where, links, _ = options[kept[n]]
        chosen.append((source, target, slot, where, links))
    return chosen, piece, parts


def colour(edges):
    at_source, at_target, result = {}, {}, {}
    degree = {}
    for source, target in edges:
        degree[("s", source)] = degree.get(("s", source), 0) + 1
        degree[("t", target)] = degree.get(("t", target), 0) + 1
    rounds = max(degree.values())
    for n, (source, target) in enumerate(edges):
        used_s = at_source.setdefault(source, {})
        used_t = at_target.setdefault(target, {})
        a = next(k for k in range(rounds) if k not in used_s)
        b = next(k for k in range(rounds) if k not in used_t)
        if a != b:
            chain, side, node, want = [], "t", target, a
            while True:
                table = at_target[node] if side == "t" else at_source[node]
                if want not in table:
                    break
                edge = table[want]
                chain.append(edge)
                node = edges[edge][0] if side == "t" else edges[edge][1]
                side = "s" if side == "t" else "t"
                want = b if want == a else a
            for edge in chain:
                s, t = edges[edge]
                del at_source[s][result[edge]], at_target[t][result[edge]]
            for edge in chain:
                s, t = edges[edge]
                result[edge] = b if result[edge] == a else a
                at_source[s][result[edge]] = edge
                at_target[t][result[edge]] = edge
        result[n] = a
        used_s[a] = n
        used_t[a] = n
    return rounds, [result[n] for n in range(len(edges))]


def pack_kernel(count, parts, lanes, step_lats, where, cov, *refs):
    outs, (straight, turned, in_sems, out_sems) = refs[:count], refs[count:]
    width = WIDTH * lanes
    span = step_lats * lanes

    def facts(p):
        row = pl.multiple_of(where[4 * p + 2] * lanes, lanes)
        col = pl.multiple_of(where[4 * p + 3] * lanes, lanes)
        used, flip = where[4 * p] == 1, where[4 * p + 1] == 1
        return used, used & flip, used & ~flip, row, col

    def copies(p, n, row, col):
        band = pl.ds(n * span, span)
        return (
            pltpu.make_async_copy(
                cov.at[pl.ds(row + n * span, span), pl.ds(col, width)],
                straight.at[p, band, :],
                in_sems.at[p, n],
            ),
            pltpu.make_async_copy(
                cov.at[pl.ds(row, width), pl.ds(col + n * span, span)],
                turned.at[p, :, band],
                in_sems.at[p, n],
            ),
            pltpu.make_async_copy(straight.at[p, band, :], outs[p].at[band, :], out_sems.at[p, n]),
        )

    for p in range(count):
        used, flipped, plain, row, col = facts(p)
        for n in range(parts):
            direct, mirror, _ = copies(p, n, row, col)
            pl.when(plain)(direct.start)
            pl.when(flipped)(mirror.start)
    for p in range(count):
        used, flipped, plain, row, col = facts(p)
        for n in range(parts):
            direct, mirror, leave = copies(p, n, row, col)
            pl.when(plain)(direct.wait)

            @pl.when(flipped)
            def _():
                mirror.wait()
                for a in range(step_lats):
                    lat = n * step_lats + a
                    rows = slice(lat * lanes, (lat + 1) * lanes)
                    for b in range(WIDTH):
                        cols = slice(b * lanes, (b + 1) * lanes)
                        straight[p, rows, cols] = turned[p, cols, rows].T

            pl.when(used)(leave.start)
    for p in range(count):
        used, flipped, plain, row, col = facts(p)
        for n in range(parts):
            pl.when(used)(copies(p, n, row, col)[2].wait)


def pack(where, cov, count, piece, lanes):
    parts = max(piece // 4, 1)
    step = piece // parts
    tall, width = piece * lanes, WIDTH * lanes
    shape = jax.ShapeDtypeStruct((tall, width), cov.dtype)
    return pl.pallas_call(
        functools.partial(pack_kernel, count, parts, lanes, step),
        out_shape=(shape,) * count,
        in_specs=[
            pl.BlockSpec(memory_space=pltpu.SMEM),
            pl.BlockSpec(memory_space=pl.ANY),
        ],
        out_specs=(pl.BlockSpec(memory_space=pl.ANY),) * count,
        scratch_shapes=[
            pltpu.VMEM((count, tall, width), cov.dtype),
            pltpu.VMEM((count, width, tall), cov.dtype),
            pltpu.SemaphoreType.DMA((count, parts)),
            pltpu.SemaphoreType.DMA((count, parts)),
        ],
        compiler_params=pltpu.CompilerParams(vmem_limit_bytes=VMEM_LIMIT),
        cost_estimate=pl.CostEstimate(
            flops=0, bytes_accessed=8 * count * tall * width, transcendentals=0
        ),
        name="pack",
    )(where, cov)


def halves(value):
    coarse = value.astype(jnp.bfloat16)
    return coarse, (value - coarse.astype(jnp.float32)).astype(jnp.bfloat16)


def row_step(strips, fields, slots, lats, row_coefs, row_mixers, half):
    source, one, two = fields
    (c0, c1, c2, c3), (f1, f2, f3), (g1, g2, g3) = slots
    lanes = row_mixers[0].shape[1] // 2
    together = 2 if strips % 2 == 0 else 1

    def stage(n, here, north, south):
        parts = [halves(h) for h in here]
        stacked = [jnp.concatenate(p, axis=0) for p in parts]
        both = jnp.dot(
            row_mixers[n][lats[n]],
            jnp.concatenate(stacked, axis=1),
            preferred_element_type=jnp.float32,
        )
        result = []
        for k in range(together):
            cols = slice(k * lanes, (k + 1) * lanes)
            value = both[:lanes, cols] + both[lanes:, cols]
            value = value + row_coefs[n][lats[n], 0] * north[k]
            result.append(value + row_coefs[n][lats[n], 1] * south[k])
        return result

    for group in range(strips // together):
        at = range(group * together, (group + 1) * together)

        def take(field, slot):
            return [field[slot, s] for s in at]

        here, mid = take(source, c1), take(source, c2)
        value = stage(0, here, take(source, c0), mid)
        v1 = [h + third * x for h, x in zip(here, value)]
        value = stage(1, take(one, f2), v1, take(one, f3))
        v2 = [m + 0.5 * x for m, x in zip(mid, value)]
        value = stage(2, take(two, g2), v2, take(two, g3))
        for s, x, y, base, z in zip(at, v1, v2, take(source, c3), value):
            one[f1, s] = x
            two[g1, s] = y
            half[s] = base + z


def ring_slots(step):
    field = [lax.rem(step + 4 - back, 4) for back in range(4)]
    one = [lax.rem(step + 6 - back, 3) for back in range(3)]
    return field, one, one


def col_stage(fields, lat, weights, mixers):
    total = None
    if lat in fields:
        here = fields[lat]
        lanes = here.shape[1]
        both = jnp.dot(
            jnp.concatenate(halves(here), axis=1),
            mixers[lat + 2],
            preferred_element_type=jnp.float32,
        )
        total = both[:, :lanes] + both[:, lanes:]
    for step, k in ((1, 2), (-1, 3)):
        if lat + step in fields:
            value = weights[lat + 2, k : k + 1, :] * fields[lat + step]
            total = value if total is None else total + value
    return total


def plus(fields, lat, value):
    return fields[lat] + value if lat in fields else value


def stream_kernel(plan, lat_col, lanes, *refs):
    sources = refs[: plan.sources]
    noise, *row_weights, col_coefs, mixers = refs[plan.sources : plan.sources + 9]
    row_coefs, row_mixers = row_weights[:3], row_weights[3:]
    out, ring, one, two, half, first, second = refs[-7:]
    step = pl.program_id(0)
    local = plan.local(step)
    slots = ring_slots(step)

    for source, when in zip(sources, plan.which(step)):

        @pl.when(when)
        def _():
            slot = slots[0][0]
            for s in range(lat_col):
                ring[slot, s] = source[:, s * lanes : (s + 1) * lanes]

    @pl.when(local >= 2)
    def _():
        row_step(lat_col, (ring, one, two), slots, [0, 0, 0], row_coefs, row_mixers, half)

    @pl.when(local >= 2 * WIDTH)
    def _():
        @pl.loop(0, lanes // COL_ROWS)
        def _(n):
            rows = pl.ds(pl.multiple_of(n * COL_ROWS, COL_ROWS), COL_ROWS)
            u = Stored(half, rows, 0, range(lat_col))
            v = Stored(first, rows, 1, [])
            w = Stored(second, rows, 1, [])
            for lat in range(-1, lat_col + 3):
                if lat <= lat_col:
                    v[lat] = plus(u, lat, third * col_stage(u, lat, col_coefs, mixers))
                at = lat - 1
                if -1 <= at <= lat_col:
                    w[at] = plus(u, at, 0.5 * col_stage(v, at, col_coefs, mixers))
                at = lat - 2
                if 0 <= at < lat_col:
                    span = slice(at * lanes, (at + 1) * lanes)
                    value = u[at] + col_stage(w, at, col_coefs, mixers)
                    out[rows, span] = value + noise[rows, span]


class Stored:
    def __init__(self, ref, rows, shift, lats):
        self.ref, self.rows, self.shift, self.lats = ref, rows, shift, set(lats)

    def __contains__(self, lat):
        return lat in self.lats

    def __getitem__(self, lat):
        return self.ref[lat + self.shift, self.rows, :]

    def __setitem__(self, lat, value):
        self.lats.add(lat)
        self.ref[lat + self.shift, self.rows, :] = value


class Inner:
    sources = 1

    def __init__(self, lats):
        self.lats = lats
        self.steps = lats

    def local(self, step):
        return step

    def lat(self, step):
        return step

    def which(self, step):
        return (step >= 0,)

    def inputs(self):
        return (lambda n: (n, 0),)

    def output(self, step):
        return (jnp.clip(step - WIDTH, WIDTH, self.lats - WIDTH - 1), 0)


class Ends:
    sources = 3

    def __init__(self, lats):
        self.lats = lats
        self.steps = 6 * WIDTH

    def local(self, step):
        return lax.rem(step, 3 * WIDTH)

    def lat(self, step):
        upper = step >= 3 * WIDTH
        return jnp.where(upper, self.lats - 5 * WIDTH + step, step - WIDTH)

    def which(self, step):
        lat = self.lat(step)
        return lat < 0, (lat >= 0) & (lat < self.lats), lat >= self.lats

    def inputs(self):
        def low(n):
            return (jnp.minimum(n, WIDTH - 1), 0)

        def own(n):
            return (jnp.clip(self.lat(n), 0, self.lats - 1), 0)

        def high(n):
            return (jnp.clip(self.lat(n) - self.lats, 0, WIDTH - 1), 0)

        return low, own, high

    def output(self, step):
        upper = step >= 3 * WIDTH
        back = jnp.maximum(self.local(step) - 2 * WIDTH, 0)
        return (jnp.where(upper, self.lats - WIDTH, 0) + back, 0)


def stream(
    plan, sources, noise, row_coefs, row_mixers, col_coefs, mixers, lanes, kept=None
):
    rows, cols = noise.shape
    lat_col = cols // lanes
    band = (lanes, cols)
    tall = (lat_col, lanes, lanes)

    def lat_spec(array, back):
        def index(n):
            return (jnp.maximum(plan.lat(n) + WIDTH - back, 0),) + (0,) * (array.ndim - 1)

        return pl.BlockSpec((1,) + array.shape[1:], index)

    extra, aliases = (), {}
    extra_specs = []
    if kept is not None:
        extra = (kept,)
        extra_specs = [pl.BlockSpec(memory_space=pl.ANY)]
        aliases = {plan.sources + 9: 0}
    work = rows * cols * plan.steps // (rows // lanes)
    return pl.pallas_call(
        functools.partial(stream_kernel, plan, lat_col, lanes),
        grid=(plan.steps,),
        out_shape=jax.ShapeDtypeStruct(noise.shape, noise.dtype),
        in_specs=[pl.BlockSpec(band, index) for index in plan.inputs()]
        + [
            pl.BlockSpec(band, plan.output),
        ]
        + [lat_spec(array, back) for array in (row_coefs, row_mixers) for back in (1, 2, 3)]
        + [
            pl.BlockSpec(memory_space=pltpu.VMEM),
            pl.BlockSpec(memory_space=pltpu.VMEM),
        ]
        + extra_specs,
        out_specs=pl.BlockSpec(band, plan.output),
        scratch_shapes=[
            pltpu.VMEM((4,) + tall, noise.dtype),
            pltpu.VMEM((3,) + tall, noise.dtype),
            pltpu.VMEM((3,) + tall, noise.dtype),
            pltpu.VMEM((lat_col, lanes, lanes), noise.dtype),
            pltpu.VMEM((lat_col + 2, lanes, lanes), noise.dtype),
            pltpu.VMEM((lat_col + 2, lanes, lanes), noise.dtype),
        ],
        input_output_aliases=aliases,
        compiler_params=pltpu.CompilerParams(
            vmem_limit_bytes=VMEM_LIMIT, dimension_semantics=("arbitrary",)
        ),
        cost_estimate=pl.CostEstimate(
            flops=70 * work, bytes_accessed=12 * work, transcendentals=0
        ),
        name=type(plan).__name__.lower(),
    )(*sources, noise, *[row_coefs] * 3, *[row_mixers] * 3, col_coefs, mixers, *extra)


def corner_kernel(count, parts, slots, *refs):
    got, (first, last, sems) = (refs[:count], refs[count : 2 * count]), refs[2 * count :]
    piece, _, width = got[0][0].shape
    ends = ((0, first, 0), (parts - 1, last, piece - WIDTH))
    for go in (0, 1):
        for side in range(2):
            for k, (part, ref, lat) in enumerate(ends):
                slot = slots[side * parts + part]
                target = ref.at[:, :, pl.ds(side * width, width)]
                for n in range(count):

                    @pl.when(slot == n)
                    def _():
                        copy = pltpu.make_async_copy(
                            got[side][n].at[pl.ds(lat, WIDTH)], target, sems.at[side, k]
                        )
                        copy.wait() if go else copy.start()

                if not go:

                    @pl.when(slot < 0)
                    def _():
                        target[...] = jnp.zeros(target.shape, target.dtype)


def corners(slots, got, parts):
    _, lanes, width = got[0].shape
    shape = jax.ShapeDtypeStruct((WIDTH, lanes, 2 * width), got[0].dtype)
    return pl.pallas_call(
        functools.partial(corner_kernel, len(got) // 2, parts),
        out_shape=(shape, shape),
        in_specs=[pl.BlockSpec(memory_space=pltpu.SMEM)]
        + [pl.BlockSpec(memory_space=pl.ANY)] * len(got),
        out_specs=(pl.BlockSpec(memory_space=pltpu.VMEM),) * 2,
        scratch_shapes=[pltpu.SemaphoreType.DMA((2, 2))],
        compiler_params=pltpu.CompilerParams(vmem_limit_bytes=VMEM_LIMIT),
        name="corners",
    )(slots, *got)


def rim_kernel(count, parts, lats, lat_col, lanes, slots, *refs):
    got = refs[:count], refs[count : 2 * count]
    low, high, coefs_hbm, mixers_hbm, col_coefs, mixers, _, out = refs[2 * count : 2 * count + 8]
    (halo, edge, row_coefs, row_mixers, one, two, half, got_sem, end_sem, in_sem, out_sem, coef_sem) = (
        refs[2 * count + 8 :]
    )
    piece = lats // parts
    width = WIDTH * lanes
    tall = lats + 2 * WIDTH
    depth = 4 if piece % 4 == 0 else piece
    segments = lats // depth
    lead = 2

    def strip_of(field, strip):
        return field.at[:, :, pl.ds(strip * lanes, lanes)]

    def place(first, strip, deep):
        return halo.at[pl.ds(first, deep), strip]

    def end_copies():
        for n in range(2 * WIDTH):
            yield pltpu.make_async_copy(strip_of(low, n), place(0, n, WIDTH), end_sem)
            yield pltpu.make_async_copy(strip_of(high, n), place(WIDTH + lats, n, WIDTH), end_sem)

    def coef_copies(first, deep, sem):
        span = pl.ds(first, deep)
        for k, (source, target) in enumerate(((coefs_hbm, row_coefs), (mixers_hbm, row_mixers))):
            yield pltpu.make_async_copy(source.at[span], target.at[span], coef_sem.at[k, sem])

    def halo_copies(segment, go):
        first = WIDTH + segment * depth
        part = (segment * depth) // piece
        for side in range(2):
            slot = slots[side * parts + part]
            for n in range(count):

                @pl.when(slot == n)
                def _():
                    inner = pl.ds(lax.rem(segment * depth, piece), depth)
                    for k in range(WIDTH):
                        copy = pltpu.make_async_copy(
                            got[side][n].at[inner, :, pl.ds(k * lanes, lanes)],
                            place(first, side * WIDTH + k, depth),
                            got_sem.at[side, segment],
                        )
                        copy.wait() if go else copy.start()

            if not go:

                @pl.when(slot < 0)
                def _():
                    @pl.loop(first, first + depth)
                    def _(lat):
                        halo[lat, side * WIDTH : (side + 1) * WIDTH] = jnp.zeros(
                            (WIDTH, lanes, lanes), halo.dtype
                        )

    def edge_copy(segment, side, inward):
        lat = pl.ds(segment * depth, depth)
        outside = out.at[lat, :, pl.ds(side * (lat_col - WIDTH) * lanes, width)]
        inside = edge.at[lat, :, pl.ds(side * width, width)]
        if inward:
            return pltpu.make_async_copy(outside, inside, in_sem.at[side, segment])
        return pltpu.make_async_copy(inside, outside, out_sem.at[side, segment])

    def segment_of_coefs(segment):
        return coef_copies(lead + segment * depth, depth, segment)

    for copy in (*end_copies(), *coef_copies(0, lead, segments)):
        copy.start()

    @pl.loop(0, segments)
    def _(segment):
        halo_copies(segment, False)
        for copy in segment_of_coefs(segment):
            copy.start()
        for side in range(2):
            edge_copy(segment, side, True).start()

    last = (lead + lats, tall - lead - lats, segments + 1)
    for copy in coef_copies(*last):
        copy.start()
    for copy in (*end_copies(), *coef_copies(0, lead, segments)):
        copy.wait()

    def arrive(step):
        segment = (step - WIDTH) // depth

        @pl.when((step >= WIDTH) & (lax.rem(step - WIDTH, depth) == 0) & (segment < segments))
        def _():
            halo_copies(segment, True)
            for copy in segment_of_coefs(segment):
                copy.wait()
            for side in range(2):
                edge_copy(segment, side, True).wait()

        @pl.when(step == WIDTH + lats)
        def _():
            for copy in coef_copies(*last):
                copy.wait()

    def rows(step):
        _, early, later = ring_slots(step)
        back = [jnp.maximum(step - n, 0) for n in range(4)]
        row_step(
            2 * WIDTH,
            (halo, one, two),
            (back, early, later),
            back[1:],
            [row_coefs] * 3,
            [row_mixers] * 3,
            half.at[lax.rem(step, 2)],
        )

    def columns(lat):
        done = half.at[lax.rem(lat, 2)]
        field = [done[n] for n in range(2 * WIDTH)]
        for side in range(2):
            def at(d):
                return d if side == 0 else lat_col - 1 - d

            base = side * WIDTH
            u = {at(d): field[base + (d + WIDTH if side == 0 else -d - 1)] for d in (-3, -2, -1)}
            v = {
                at(d): plus(u, at(d), third * col_stage(u, at(d), col_coefs, mixers))
                for d in (-2, -1, 0)
            }
            w = {
                at(d): plus(u, at(d), 0.5 * col_stage(v, at(d), col_coefs, mixers))
                for d in (-1, 0, 1)
            }
            for d in range(WIDTH):
                start = side * width + (d if side == 0 else WIDTH - 1 - d) * lanes
                span = slice(start, start + lanes)
                value = col_stage(w, at(d), col_coefs, mixers)
                edge[lat, :, span] = edge[lat, :, span] + value

    warm = 2 * WIDTH + 1

    @pl.loop(2, warm)
    def _(step):
        arrive(step)
        rows(step)

    def leave(segment):
        for side in range(2):
            edge_copy(segment, side, False).start()

    @pl.loop(warm, tall)
    def _(step):
        arrive(step)
        lat = step - warm
        columns(lat)
        rows(step)

        @pl.when(lax.rem(lat, depth) == depth - 1)
        def _():
            leave(lat // depth)

    columns(lats - 1)
    leave(segments - 1)
    for segment in range(segments):
        for side in range(2):
            edge_copy(segment, side, False).wait()


def rim(
    slots, got, low, high, row_coefs, row_mixers, col_coefs, mixers, forecast, parts, lanes
):
    rows, cols = forecast.shape
    lats, lat_col = rows // lanes, cols // lanes
    count = len(got) // 2
    width = WIDTH * lanes
    kept = forecast.reshape(lats, lanes, cols)
    tall = (2 * WIDTH, lanes, lanes)
    anywhere = pl.BlockSpec(memory_space=pl.ANY)
    vmem = pl.BlockSpec(memory_space=pltpu.VMEM)
    result = pl.pallas_call(
        functools.partial(rim_kernel, count, parts, lats, lat_col, lanes),
        out_shape=jax.ShapeDtypeStruct(kept.shape, kept.dtype),
        in_specs=[pl.BlockSpec(memory_space=pltpu.SMEM)]
        + [anywhere] * (2 * count + 4)
        + [vmem, vmem, anywhere],
        out_specs=anywhere,
        scratch_shapes=[
            pltpu.VMEM((lats + 2 * WIDTH,) + tall, kept.dtype),
            pltpu.VMEM((lats, lanes, 2 * width), kept.dtype),
            pltpu.VMEM(row_coefs.shape, row_coefs.dtype),
            pltpu.VMEM(row_mixers.shape, row_mixers.dtype),
            pltpu.VMEM((3,) + tall, kept.dtype),
            pltpu.VMEM((3,) + tall, kept.dtype),
            pltpu.VMEM((2,) + tall, kept.dtype),
            pltpu.SemaphoreType.DMA((2, lats)),
            pltpu.SemaphoreType.DMA,
            pltpu.SemaphoreType.DMA((2, lats)),
            pltpu.SemaphoreType.DMA((2, lats)),
            pltpu.SemaphoreType.DMA((2, lats + 2)),
        ],
        input_output_aliases={1 + 2 * count + 6: 0},
        compiler_params=pltpu.CompilerParams(vmem_limit_bytes=VMEM_LIMIT),
        cost_estimate=pl.CostEstimate(
            flops=13 * rows * cols, bytes_accessed=20 * rows * width, transcendentals=0
        ),
        name="rim",
    )(slots, *got, low, high, row_coefs, row_mixers, col_coefs, mixers, kept)
    return result.reshape(rows, cols)


def coefficients(velocity_x, velocity_y, diffusion, start, count, reach):
    stack = jnp.stack(
        [
            diffusion - 0.5 * velocity_x,
            diffusion + 0.5 * velocity_x,
            diffusion - 0.5 * velocity_y,
            diffusion + 0.5 * velocity_y,
            -4.0 * diffusion,
        ],
        axis=1,
    )
    padded = jnp.pad(stack, ((reach, reach), (0, 0), (0, 0)))
    return lax.dynamic_slice_in_dim(padded, start, count + 2 * reach, 0)


def circulants(coefs, side):
    lanes = coefs.shape[-1]
    source = lax.broadcasted_iota(jnp.int32, (lanes, lanes), 1 - side)
    target = lax.broadcasted_iota(jnp.int32, (lanes, lanes), side)
    apart = jnp.mod(source - target, lanes)
    shape = (coefs.shape[0], 1, lanes) if side else (coefs.shape[0], lanes, 1)
    east, west, here = (coefs[:, k, :].reshape(shape) for k in (0, 1, 4))
    matrix = jnp.where(apart == 1, east, 0.0) + jnp.where(apart == lanes - 1, west, 0.0)
    matrix = matrix + jnp.where(apart == 0, here, 0.0)
    coarse = lax.reduce_precision(matrix, 8, 7)
    both = jnp.concatenate([coarse, matrix - coarse], axis=1 + side).astype(jnp.bfloat16)
    return jnp.concatenate([both, both], axis=2 - side)


def solution(mesh):
    rows, cols = mesh.shape["row"], mesh.shape["col"]

    def shards(cov, noise, velocity_x, velocity_y, diffusion):
        lanes = velocity_x.shape[1]
        tile_rows, tile_cols = cov.shape
        lat_row, lat_col = tile_rows // lanes, tile_cols // lanes
        chosen, piece, parts = halo_plan(rows, cols, lat_row, lat_col)
        row, col = lax.axis_index("row"), lax.axis_index("col")
        here = row * cols + col

        def flat(place):
            return place[0] * cols + place[1]

        def mine(table):
            return lax.dynamic_index_in_dim(jnp.array(table, jnp.int32), here, 0, False)

        sides = []
        for side in range(2):
            jobs = [job for job in chosen if job[2][0] == side]
            away = [job for job in jobs if job[0] != job[1]]
            rounds, order = colour([(job[0], job[1]) for job in away])
            order = order + [rounds] * (len(jobs) - len(away))
            send = [[0] * (4 * (rounds + 1)) for _ in range(rows * cols)]
            slots = [[-1] * parts for _ in range(rows * cols)]
            pairs = [[] for _ in range(rounds)]
            for job, n in zip(away + [job for job in jobs if job[0] == job[1]], order):
                source, target, (_, part), where, _ = job
                send[flat(source)][4 * n : 4 * n + 4] = [1, *where]
                slots[flat(target)][part] = n
                if n < rounds:
                    pairs[n].append((flat(source), flat(target)))
            sides.append((rounds, mine(send), mine(slots), pairs))

        up = [(r, r + 1) for r in range(rows - 1)]
        down = [(b, a) for a, b in up]
        reach = WIDTH * lanes
        top, bottom = cov[tile_rows - reach :], cov[:reach]
        low = lax.ppermute(top, "row", up)
        high = lax.ppermute(bottom, "row", down)
        got = []
        ahead = (top, bottom)
        for rounds, send, _, pairs in sides:
            send, *ahead = lax.optimization_barrier((send, *ahead))
            packed = pack(send, cov, rounds + 1, piece, lanes)
            ahead = [packed[-1]]
            moved = [lax.ppermute(v, ("row", "col"), p) for v, p in zip(packed, pairs)]
            got.append([v.reshape(piece, lanes, reach) for v in [*moved, packed[-1]]])

        narrow = coefficients(
            velocity_x, velocity_y, diffusion, row * lat_row, lat_row, WIDTH
        )
        row_mixers = circulants(narrow, 0)
        narrow = narrow[:, 2:4, :, None]
        row_coefs = jnp.broadcast_to(narrow, narrow.shape[:3] + (lanes,))
        col_coefs = coefficients(velocity_x, velocity_y, diffusion, col * lat_col, lat_col, 2)
        mixers = circulants(col_coefs, 1)
        forecast = stream(
            Inner(lat_row), (cov,), noise, row_coefs, row_mixers, col_coefs, mixers, lanes
        )
        low, high, forecast = lax.optimization_barrier((low, high, forecast))
        forecast = stream(
            Ends(lat_row),
            (low, cov, high),
            noise,
            row_coefs,
            row_mixers,
            col_coefs,
            mixers,
            lanes,
            forecast,
        )
        most = max(len(buffers) for buffers in got)
        got = [[*buffers, *[buffers[-1]] * (most - len(buffers))] for buffers in got]
        forecast, *pieces = lax.optimization_barrier((forecast, *got[0], *got[1]))
        slots = jnp.concatenate([slots for _, _, slots, _ in sides])
        first, last = corners(slots, pieces, parts)
        low = lax.ppermute(last, "row", up)
        high = lax.ppermute(first, "row", down)
        forecast = rim(
            slots,
            pieces,
            low,
            high,
            row_coefs,
            row_mixers,
            col_coefs,
            mixers,
            forecast,
            parts,
            lanes,
        )
        return forecast

    spec = P("row", "col")
    return jax.shard_map(
        shards,
        mesh=mesh,
        in_specs=(spec, spec, P(), P(), P()),
        out_specs=spec,
        check_vma=False,
    )
```
